32 devices in a mesh: blk: 4 (over y, x), rep: 8 (over z, core).
Axes of the slice: x: 2, y: 2, z: 4, core: 2. Of those that a mesh axis runs over, the one named last changes fastest.
Arguments:
- image_feats: bfloat16 [8, 2048, 1024], P('rep', 'blk'), may hold values from -6 to 6
- text_feats: bfloat16 [8, 2048, 768], P('rep', 'blk'), may hold values from -6 to 6
- image_head: bfloat16 [1024, 768], replicated, may hold values from -0.1875 to 0.1875
- text_head: bfloat16 [768, 768], replicated, may hold values from -0.21875 to 0.21875
- image_lse: float32 [8, 2048], P('rep', 'blk'), as said below
- text_lse: float32 [8, 2048], P('rep', 'blk'), as said below
Outputs:
- image_feat_grad: float32 [8, 2048, 1024], P('rep', 'blk')
- text_feat_grad: float32 [8, 2048, 768], P('rep', 'blk')
- image_head_grad: float32 [1024, 768], replicated
- text_head_grad: float32 [768, 768], replicated
The draws below stay inside these ranges and needn't reach their ends.
Inputs may be any that keep to these rules, and one draw needn't show every extreme that they name: `image_lse`: each entry lies between ln(2048) + 1 and ln(2048) + 2.5. `text_lse`: each entry lies between ln(2048) + 1 and ln(2048) + 2.5.
All inputs are finite; a program needn't handle non-finite values.
Results may differ from the reference program's by a relative error of at most 0.028.
Values may be sent and summed in bfloat16 or wider, within the bound.
A program may use at most 128 MiB of HBM per device.

```python
import jax
import jax.numpy as jnp
from jax import lax

EMBED = 768
VIS_WIDTH = 1024
TXT_WIDTH = 768
PAIRS = 2048
GROUPS = 8


def normalizer_values(key, salt):
    base = jax.random.fold_in(key, salt)
    lowest = jnp.log(jnp.float32(PAIRS)) + 1.0
    pick = jax.random.uniform(jax.random.fold_in(base, 1), (GROUPS, PAIRS), jnp.float32)
    offset = 1.5 * pick
    return lowest + offset


def draw_image_lse(key, part):
    return normalizer_values(key, 11)


def draw_text_lse(key, part):
    return normalizer_values(key, 23)


def shard_levels(key, extent, cuts, least, largest):
    level, own = 1.0, jax.random.fold_in(key, 6)
    for dim, parts in cuts:
        heights = jnp.exp(jax.random.uniform(jax.random.fold_in(own, dim), (parts,), jnp.float32, least / len(cuts), largest / len(cuts)))
        level = level * jnp.repeat(heights, extent[dim] // parts).reshape([-1 if axis == dim else 1 for axis in range(len(extent))])
    return level


def normal_values(key, shape, scale, bound, pieces=(), held_as=jnp.bfloat16):
    result = jax.random.normal(key, shape, jnp.float32) * scale
    if len(pieces) > 0:
        result = shard_levels(key, shape, pieces, -0.22, 0.18) * result
    return jnp.clip(result, min=-bound, max=bound).astype(held_as)


def setup_inputs(seed: int = 0) -> dict:
    keys = jax.random.split(jax.random.key(seed), 7)
    return {
        "image_feats": normal_values(keys[0], (GROUPS, PAIRS, VIS_WIDTH), 1.0, 6.0, ((0, 8), (1, 4))),
        "text_feats": normal_values(keys[1], (GROUPS, PAIRS, TXT_WIDTH), 1.0, 6.0, ((0, 8), (1, 4))),
        "image_head": normal_values(keys[2], (VIS_WIDTH, EMBED), VIS_WIDTH ** -0.5, 0.1875),
        "text_head": normal_values(keys[3], (TXT_WIDTH, EMBED), TXT_WIDTH ** -0.5, 0.21875),
        "image_lse": draw_image_lse(jax.random.fold_in(keys[6], 71), 0),
        "text_lse": draw_text_lse(jax.random.fold_in(keys[6], 71), 0),
    }


logit_scale = 50.0
epsilon = 1e-06

def project_head(feats, weight):
    raw = jnp.dot(feats, weight, preferred_element_type=jnp.float32)
    factor = lax.rsqrt(lax.optimization_barrier(jnp.sum(raw * raw, axis=1, keepdims=True)) + epsilon)
    return (raw * factor, factor)

def pre_gradient(embed, factor, grad):
    inner = lax.optimization_barrier(jnp.sum(embed * grad, axis=1, keepdims=True))
    return (factor * (grad - embed * inner)).astype(jnp.bfloat16)

def group_grads(group):
    image_rows, text_rows, image_head, text_head, lse_img, lse_txt = group
    image_embed, image_scale = project_head(image_rows, image_head)
    text_embed, text_scale = project_head(text_rows, text_head)
    image_round = image_embed.astype(jnp.bfloat16)
    text_round = text_embed.astype(jnp.bfloat16)
    scores = logit_scale * lax.dot_general(image_round, text_round, (((1,), (1,)), ((), ())), preferred_element_type=jnp.float32)
    weights = (0.5 * (jnp.exp(scores - lse_img[:, None]) + jnp.exp(scores - lse_txt[None, :]))).astype(jnp.bfloat16)
    image_sum = jnp.dot(weights, text_round, preferred_element_type=jnp.float32)
    text_sum = lax.dot_general(weights, image_round, (((0,), (0,)), ((), ())), preferred_element_type=jnp.float32)
    image_grad = logit_scale * image_sum - logit_scale * text_round.astype(jnp.float32)
    text_grad = logit_scale * text_sum - logit_scale * image_round.astype(jnp.float32)
    image_pre = pre_gradient(image_embed, image_scale, image_grad)
    text_pre = pre_gradient(text_embed, text_scale, text_grad)
    image_back = lax.dot_general(image_pre, image_head, (((1,), (1,)), ((), ())), preferred_element_type=jnp.float32)
    text_back = lax.dot_general(text_pre, text_head, (((1,), (1,)), ((), ())), preferred_element_type=jnp.float32)
    image_wgrad = lax.dot_general(image_rows, image_pre, (((0,), (0,)), ((), ())), preferred_element_type=jnp.float32)
    text_wgrad = lax.dot_general(text_rows, text_pre, (((0,), (0,)), ((), ())), preferred_element_type=jnp.float32)
    return (image_back, text_back, image_wgrad, text_wgrad)

def reference(image_feats, text_feats, image_head, text_head, image_lse, text_lse):

    def single(index):
        group = (image_feats[index], text_feats[index], image_head, text_head, image_lse[index], text_lse[index])
        return group_grads(group)
    image_back, text_back, image_wgrad, text_wgrad = lax.map(single, jnp.arange(GROUPS, dtype=jnp.int32))
    return (image_back, text_back, lax.optimization_barrier(jnp.sum(image_wgrad, axis=0)), lax.optimization_barrier(jnp.sum(text_wgrad, axis=0)))
```

```python
import functools

import jax
import jax.numpy as jnp
from jax import lax
from jax.experimental import pallas as pl
from jax.experimental.pallas import tpu as pltpu
from jax.sharding import PartitionSpec as P

logit_scale = 50.0
epsilon = 1e-06


def project_head(feats, weight):
    raw = jnp.dot(feats, weight, preferred_element_type=jnp.float32)
    factor = lax.rsqrt(jnp.sum(raw * raw, axis=1, keepdims=True) + epsilon)
    return (raw * factor, factor)


def pre_gradient(embed, factor, grad):
    inner = jnp.sum(embed * grad, axis=1, keepdims=True)
    return (factor * (grad - embed * inner)).astype(jnp.bfloat16)


def weight_tile(left, left_lse, right, right_lse):
    scores = logit_scale * lax.dot_general(
        left, right, (((1,), (1,)), ((), ())), preferred_element_type=jnp.float32
    )
    return (
        0.5 * (jnp.exp(scores - left_lse[:, None]) + jnp.exp(scores - right_lse[None, :]))
    ).astype(jnp.bfloat16)


def shards(image_feats, text_feats, image_head, text_head, image_lse, text_lse):
    image_rows = image_feats[0]
    text_rows = text_feats[0]
    lse_img = image_lse[0]
    lse_txt = text_lse[0]
    image_embed, image_scale = project_head(image_rows, image_head)
    text_embed, text_scale = project_head(text_rows, text_head)
    image_round = image_embed.astype(jnp.bfloat16)
    text_round = text_embed.astype(jnp.bfloat16)
    image_piece = lax.all_gather(image_round, "blk", axis=0, tiled=True)
    image_piece_lse = lax.all_gather(
        lse_img.astype(jnp.bfloat16), "blk", axis=0, tiled=True
    ).astype(jnp.float32)
    text_piece = lax.all_gather(text_round, "blk", axis=0, tiled=True)
    text_piece_lse = lax.all_gather(lse_txt.astype(jnp.bfloat16), "blk", axis=0, tiled=True).astype(
        jnp.float32
    )
    image_weights = weight_tile(image_round, lse_img, text_piece, text_piece_lse)
    image_total_part = jnp.dot(image_weights, text_piece, preferred_element_type=jnp.float32)
    text_weights = weight_tile(image_piece, image_piece_lse, text_round, lse_txt)
    text_total_part = lax.dot_general(
        text_weights, image_piece, (((0,), (0,)), ((), ())), preferred_element_type=jnp.float32
    )
    image_grad = logit_scale * image_total_part - logit_scale * text_round.astype(jnp.float32)
    text_grad = logit_scale * text_total_part - logit_scale * image_round.astype(jnp.float32)
    image_pre = pre_gradient(image_embed, image_scale, image_grad)
    text_pre = pre_gradient(text_embed, text_scale, text_grad)
    image_back = lax.dot_general(
        image_pre, image_head, (((1,), (1,)), ((), ())), preferred_element_type=jnp.float32
    )
    text_back = lax.dot_general(
        text_pre, text_head, (((1,), (1,)), ((), ())), preferred_element_type=jnp.float32
    )
    image_wgrad = lax.dot_general(
        image_rows, image_pre, (((0,), (0,)), ((), ())), preferred_element_type=jnp.float32
    )
    text_wgrad = lax.dot_general(
        text_rows, text_pre, (((0,), (0,)), ((), ())), preferred_element_type=jnp.float32
    )
    image_total, text_total = lax.psum((image_wgrad, text_wgrad), ("blk", "rep"))
    return (image_back[None], text_back[None], image_total, text_total)


MESH = pl.DeviceIdType.MESH
SIDE = 2
NT = (((1,), (1,)), ((), ()))
TN = (((0,), (0,)), ((), ()))


def mm(a, b, dims=(((1,), (0,)), ((), ()))):
    return lax.dot_general(a, b, dims, preferred_element_type=jnp.float32)


def fused(
    nz, chunk,
    xi, xt, wi, wt, li, lt,
    pre_i, pre_t, hi, ht,
    ei, et, fi, ft, im, ip, tm, tp, lip, ltp, u, v, w,
    ps_i, pr_i, ps_t, pr_t, acc_i, acc_t, xit, xtt,
    out_half, own, from_core, r1, r2, r3, full,
    send, recv,
):
    n, e = im.shape
    di, dt = wi.shape[0], wt.shape[0]
    count = n // chunk
    b, r = lax.axis_index("blk"), lax.axis_index("rep")
    x, y = lax.rem(b, 2), b // 2
    core, z = lax.rem(r, 2), r // 2
    px = {"blk": y * 2 + 1 - x, "rep": r}
    py = {"blk": (1 - y) * 2 + x, "rep": r}
    pc = {"blk": b, "rep": z * 2 + 1 - core}
    pz = [{"blk": b, "rep": lax.rem(z + k, nz) * 2 + core} for k in range(1, nz)]

    used = [0]

    def push(src, dst, dev):
        s = used[0]
        used[0] += 1
        copy = pltpu.make_async_remote_copy(
            src_ref=src, dst_ref=dst, send_sem=send.at[s], recv_sem=recv.at[s],
            device_id=dev, device_id_type=MESH,
        )
        copy.start()
        started.append(copy)
        return copy

    started = []
    barrier = pltpu.get_barrier_semaphore()
    for dev in [px, py, pc] + pz:
        pl.semaphore_signal(barrier, inc=1, device_id=dev, device_id_type=MESH)

    def project(c, feats, head, embed, factor, rounded):
        rows = pl.ds(c * chunk, chunk)
        raw = mm(feats[rows, :], head[...])
        f = lax.rsqrt(jnp.sum(raw * raw, axis=1, keepdims=True) + epsilon)
        out = raw * f
        embed[rows, :] = out
        factor[rows, :] = f
        rounded[rows, :] = out.astype(jnp.bfloat16)

    got_i, got_t = [], []
    for c in range(count):
        rows = pl.ds(c * chunk, chunk)
        project(c, xi, wi, ei, fi, im)
        if c == 0:
            pl.semaphore_wait(barrier, 2 + nz)
            got_li = push(li, lip, px)
            got_lt = push(lt, ltp, py)
        got_i.append(push(im.at[rows, :], ip.at[rows, :], px))
        project(c, xt, wt, et, ft, tm)
        got_t.append(push(tm.at[rows, :], tp.at[rows, :], py))

    def columns(lse):
        half = 0.5 * jnp.exp(-lse)
        return jnp.transpose(jnp.broadcast_to(half, (128, n)))

    u[0] = columns(li[...])
    v[0] = 0.5 * jnp.exp(-lt[...])
    images, texts = (im, ip), (tm, tp)

    def tile(p, q, r0, nr, c0, nc):
        s = logit_scale * mm(images[p][pl.ds(r0, nr), :], texts[q][pl.ds(c0, nc), :], NT)
        fac = u[p, pl.ds(r0, nr), :][:, :1] + v[q, :, pl.ds(c0, nc)]
        w[p, q, pl.ds(r0, nr), pl.ds(c0, nc)] = (jnp.exp(s) * fac).astype(jnp.bfloat16)

    @pl.loop(0, count)
    def _(c):
        tile(0, 0, pl.multiple_of(c * chunk, chunk), chunk, 0, n)

    @pl.loop(0, count)
    def _(c):
        rows = pl.ds(pl.multiple_of(c * chunk, chunk), chunk)
        acc_i[rows, :] = mm(w[0, 0, rows, :], tm[...])
        acc_t[rows, :] = mm(w[0, 0, :, rows], im[...], TN)

    for src, dst, width in ((xi, xit, di), (xt, xtt, dt)):

        @pl.loop(0, width // 128)
        def _(k, src=src, dst=dst):
            part = pl.ds(pl.multiple_of(k * 128, 128), 128)
            dst[part, :] = jnp.transpose(src[:, part])

    got_li.wait_recv()
    got_lt.wait_recv()
    u[1] = columns(lip[...])
    v[1] = 0.5 * jnp.exp(-ltp[...])
    for c in range(count):
        got_i[c].wait_recv()
        tile(1, 0, c * chunk, chunk, 0, n)
        got_t[c].wait_recv()

        tile(0, 1, 0, n, c * chunk, chunk)

    sum_i, sum_t = [], []
    for c in range(count):
        rows = pl.ds(c * chunk, chunk)
        tile(1, 1, c * chunk, chunk, 0, n)
        ps_i[rows, :] = (mm(w[1, 0, rows, :], tm[...]) + mm(w[1, 1, rows, :], tp[...])).astype(
            jnp.bfloat16
        )
        sum_i.append(push(ps_i.at[rows, :], pr_i.at[rows, :], px))
    for c in range(count):
        rows = pl.ds(c * chunk, chunk)
        ps_t[rows, :] = (
            mm(w[0, 1, :, rows], im[...], TN) + mm(w[1, 1, :, rows], ip[...], TN)
        ).astype(jnp.bfloat16)
        sum_t.append(push(ps_t.at[rows, :], pr_t.at[rows, :], py))

    @pl.loop(0, count)
    def _(c):
        rows = pl.ds(pl.multiple_of(c * chunk, chunk), chunk)
        acc_i[rows, :] += mm(w[0, 1, rows, :], tp[...])
        acc_t[rows, :] += mm(w[1, 0, :, rows], ip[...], TN)

    def finish(c, acc, part, other, embed, factor, out):
        rows = pl.ds(c * chunk, chunk)
        total = acc[rows, :] + part[rows, :].astype(jnp.float32)
        grad = logit_scale * total - logit_scale * other[rows, :].astype(jnp.float32)
        out[rows, :] = pre_gradient(embed[rows, :], factor[rows, :], grad)

    for c in range(count):
        sum_i[c].wait_recv()
        finish(c, acc_i, pr_i, tm, ei, fi, pre_i)
        sum_t[c].wait_recv()
        finish(c, acc_t, pr_t, im, et, ft, pre_t)

    eh = e // 2
    bi, bt = di // (8 * nz), dt // (8 * nz)

    def head_half(which, dst):
        for q in range(4):
            rows = pl.ds(pl.multiple_of(which * (di // 2) + q * nz * bi, nz * bi), nz * bi)
            g = mm(xit[rows, :], pre_i[...]).astype(jnp.bfloat16)
            for ab in range(2):
                for k in range(nz):
                    dst[ab, q // 2, q % 2, k, 0:bi, :] = g[k * bi : (k + 1) * bi, ab * eh : (ab + 1) * eh]
            rows = pl.ds(pl.multiple_of(which * (dt // 2) + q * nz * bt, nz * bt), nz * bt)
            g = mm(xtt[rows, :], pre_t[...])
            for ab in range(2):
                for k in range(nz):
                    dst[ab, q // 2, q % 2, k, bi : bi + bt, :] = g[
                        k * bt : (k + 1) * bt, ab * eh : (ab + 1) * eh
                    ].astype(jnp.bfloat16)

    def added(p, q):
        return (p.astype(jnp.float32) + q.astype(jnp.float32)).astype(jnp.bfloat16)

    ij = ((x, y), (y, x))
    pi, pj = (px, py), (py, px)
    head_half(1 - core, out_half)
    first = [push(out_half.at[ab, 1 - ij[ab][0]], from_core.at[ab, 1 - ij[ab][0]], pc) for ab in range(2)]
    second = [push(out_half.at[ab, ij[ab][0]], from_core.at[ab, ij[ab][0]], pc) for ab in range(2)]
    head_half(core, own)
    s1 = []
    for ab in range(2):
        i = ij[ab][0]
        first[ab].wait_recv()
        own[ab, 1 - i] = added(own[ab, 1 - i], from_core[ab, 1 - i])
        s1.append(push(own.at[ab, 1 - i], r1.at[ab], pi[ab]))
    for ab in range(2):
        i = ij[ab][0]
        second[ab].wait_recv()
        own[ab, i] = added(own[ab, i], from_core[ab, i])
    s2 = []
    for ab in range(2):
        i, j = ij[ab]
        s1[ab].wait_recv()
        own[ab, i] = added(own[ab, i], r1[ab])
        s2.append(push(own.at[ab, i, 1 - j], r2.at[ab], pj[ab]))
    s3 = []
    for ab in range(2):
        i, j = ij[ab]
        s2[ab].wait_recv()
        own[ab, i, j] = added(own[ab, i, j], r2[ab])
        s3.append(
            [push(own.at[ab, i, j, lax.rem(z + k, nz)], r3.at[ab, k], pz[k - 1]) for k in range(1, nz)]
        )
    s4 = []
    for ab in range(2):
        i, j = ij[ab]
        total = own[ab, i, j, z].astype(jnp.float32)
        for k in range(1, nz):
            s3[ab][k - 1].wait_recv()
            total = total + r3[ab, k].astype(jnp.float32)
        full[core, ab, i, j, z] = total.astype(jnp.bfloat16)
        piece = full.at[core, ab, i, j, z]
        s4.append([push(piece, piece, pz[k - 1]) for k in range(1, nz)])
    s5 = []
    for ab in range(2):
        i, j = ij[ab]
        for copy in s4[ab]:
            copy.wait_recv()
        piece = full.at[core, ab, i, j]
        s5.append(push(piece, piece, pj[ab]))
    s6, last = [], []
    for ab in range(2):
        i, j = ij[ab]
        s5[ab].wait_recv()
        piece = full.at[core, ab, i]
        s6.append(push(piece, piece, pi[ab]))
        last.append(push(piece, piece, pc))
    for ab in range(2):
        i, j = ij[ab]
        s6[ab].wait_recv()
        piece = full.at[core, ab, 1 - i]
        last.append(push(piece, piece, pc))
    for copy in last:
        copy.wait_recv()
    for cc in range(2):
        for ab in range(2):
            for q in range(4):
                for k in range(nz):
                    p = q * nz + k
                    cols = pl.ds(ab * eh, eh)
                    piece = full[cc, ab, q // 2, q % 2, k]
                    hi[pl.ds(cc * (di // 2) + p * bi, bi), cols] = piece[:bi]
                    ht[pl.ds(cc * (dt // 2) + p * bt, bt), cols] = piece[bi:]
    for copy in started:
        copy.wait_send()


def kernel_shards(nz, image_feats, text_feats, image_head, text_head, image_lse, text_lse):
    n, di = image_feats.shape[1:]
    dt, e = text_head.shape
    chunk = n // 4
    bf, f32 = jnp.bfloat16, jnp.float32
    pr, eh = (di + dt) // (8 * nz), e // 2
    vm = pltpu.VMEM
    pieces = lambda *lead: vm((*lead, pr, eh), bf)
    copies = 2 + 4 * (n // chunk) + 4 + 2 + 2 + 2 * (nz - 1) * 2 + 2 + 2 + 4
    spec = pl.BlockSpec(memory_space=pltpu.VMEM)
    pre_i, pre_t, hi, ht = pl.pallas_call(
        functools.partial(fused, nz, chunk),
        out_shape=[
            jax.ShapeDtypeStruct((n, e), bf),
            jax.ShapeDtypeStruct((n, e), bf),
            jax.ShapeDtypeStruct((di, e), bf),
            jax.ShapeDtypeStruct((dt, e), bf),
        ],
        in_specs=[spec] * 6,
        out_specs=[spec] * 4,
        scratch_shapes=[
            vm((n, e), f32), vm((n, e), f32), vm((n, 1), f32), vm((n, 1), f32),
            vm((n, e), bf), vm((n, e), bf), vm((n, e), bf), vm((n, e), bf),
            vm((1, n), f32), vm((1, n), f32), vm((2, n, 128), f32), vm((2, 1, n), f32),
            vm((2, 2, n, n), bf),
            vm((n, e), bf), vm((n, e), bf), vm((n, e), bf), vm((n, e), bf),
            vm((n, e), f32), vm((n, e), f32), vm((di, n), bf), vm((dt, n), bf),
            pieces(2, 2, 2, nz), pieces(2, 2, 2, nz), pieces(2, 2, 2, nz),
            pieces(2, 2, nz), pieces(2, nz), pieces(2, nz), pieces(2, 2, 2, 2, nz),
            pltpu.SemaphoreType.DMA((copies,)), pltpu.SemaphoreType.DMA((copies,)),
        ],
        compiler_params=pltpu.CompilerParams(
            collective_id=0, has_side_effects=True, vmem_limit_bytes=60 * 1024 * 1024
        ),
    )(image_feats[0], text_feats[0], image_head, text_head, image_lse, text_lse)
    image_back = lax.dot_general(pre_i, image_head, NT, preferred_element_type=f32)
    text_back = lax.dot_general(pre_t, text_head, NT, preferred_element_type=f32)
    return (image_back[None], text_back[None], hi.astype(f32), ht.astype(f32))


def solution(mesh):
    blk, rep = mesh.shape["blk"], mesh.shape["rep"]
    body = shards
    if blk == SIDE * SIDE and rep % SIDE == 0:
        body = functools.partial(kernel_shards, rep // SIDE)
    return jax.shard_map(
        body,
        mesh=mesh,
        in_specs=(
            P("rep", "blk", None),
            P("rep", "blk", None),
            P(),
            P(),
            P("rep", "blk"),
            P("rep", "blk"),
        ),
        out_specs=(P("rep", "blk", None), P("rep", "blk", None), P(), P()),
        check_vma=False,
    )
```

```python
import functools

import jax
import jax.numpy as jnp
from jax import lax
from jax.experimental import pallas as pl
from jax.experimental.pallas import tpu as pltpu
from jax.sharding import PartitionSpec as P

logit_scale = 50.0
epsilon = 1e-06


def project_head(feats, weight):
    raw = jnp.dot(feats, weight, preferred_element_type=jnp.float32)
    factor = lax.rsqrt(jnp.sum(raw * raw, axis=1, keepdims=True) + epsilon)
    return (raw * factor, factor)


def pre_gradient(embed, factor, grad):
    inner = jnp.sum(embed * grad, axis=1, keepdims=True)
    return (factor * (grad - embed * inner)).astype(jnp.bfloat16)


def weight_tile(left, left_lse, right, right_lse):
    scores = logit_scale * lax.dot_general(
        left, right, (((1,), (1,)), ((), ())), preferred_element_type=jnp.float32
    )
    return (
        0.5 * (jnp.exp(scores - left_lse[:, None]) + jnp.exp(scores - right_lse[None, :]))
    ).astype(jnp.bfloat16)


def shards(image_feats, text_feats, image_head, text_head, image_lse, text_lse):
    image_rows = image_feats[0]
    text_rows = text_feats[0]
    lse_img = image_lse[0]
    lse_txt = text_lse[0]
    image_embed, image_scale = project_head(image_rows, image_head)
    text_embed, text_scale = project_head(text_rows, text_head)
    image_round = image_embed.astype(jnp.bfloat16)
    text_round = text_embed.astype(jnp.bfloat16)
    image_piece = lax.all_gather(image_round, "blk", axis=0, tiled=True)
    image_piece_lse = lax.all_gather(
        lse_img.astype(jnp.bfloat16), "blk", axis=0, tiled=True
    ).astype(jnp.float32)
    text_piece = lax.all_gather(text_round, "blk", axis=0, tiled=True)
    text_piece_lse = lax.all_gather(lse_txt.astype(jnp.bfloat16), "blk", axis=0, tiled=True).astype(
        jnp.float32
    )
    image_weights = weight_tile(image_round, lse_img, text_piece, text_piece_lse)
    image_total_part = jnp.dot(image_weights, text_piece, preferred_element_type=jnp.float32)
    text_weights = weight_tile(image_piece, image_piece_lse, text_round, lse_txt)
    text_total_part = lax.dot_general(
        text_weights, image_piece, (((0,), (0,)), ((), ())), preferred_element_type=jnp.float32
    )
    image_grad = logit_scale * image_total_part - logit_scale * text_round.astype(jnp.float32)
    text_grad = logit_scale * text_total_part - logit_scale * image_round.astype(jnp.float32)
    image_pre = pre_gradient(image_embed, image_scale, image_grad)
    text_pre = pre_gradient(text_embed, text_scale, text_grad)
    image_back = lax.dot_general(
        image_pre, image_head, (((1,), (1,)), ((), ())), preferred_element_type=jnp.float32
    )
    text_back = lax.dot_general(
        text_pre, text_head, (((1,), (1,)), ((), ())), preferred_element_type=jnp.float32
    )
    image_wgrad = lax.dot_general(
        image_rows, image_pre, (((0,), (0,)), ((), ())), preferred_element_type=jnp.float32
    )
    text_wgrad = lax.dot_general(
        text_rows, text_pre, (((0,), (0,)), ((), ())), preferred_element_type=jnp.float32
    )
    image_total, text_total = lax.psum((image_wgrad, text_wgrad), ("blk", "rep"))
    return (image_back[None], text_back[None], image_total, text_total)


MESH = pl.DeviceIdType.MESH
SIDE = 2
NT = (((1,), (1,)), ((), ()))
TN = (((0,), (0,)), ((), ()))


def mm(a, b, dims=(((1,), (0,)), ((), ()))):
    return lax.dot_general(a, b, dims, preferred_element_type=jnp.float32)


def fused(
    nz, chunk,
    xi, xt, wi, wt, li, lt,
    pre_i, pre_t, hi, ht,
    ei, et, fi, ft, im, ip, tm, tp, lip, ltp, u, v, w,
    ps_i, pr_i, ps_t, pr_t, acc_i, acc_t, xit, xtt,
    bufs_i, bufs_t,
    send, recv,
):
    n, e = im.shape
    di, dt = wi.shape[0], wt.shape[0]
    count = n // chunk
    b, r = lax.axis_index("blk"), lax.axis_index("rep")
    x, y = lax.rem(b, 2), b // 2
    core, z = lax.rem(r, 2), r // 2
    px = {"blk": y * 2 + 1 - x, "rep": r}
    py = {"blk": (1 - y) * 2 + x, "rep": r}
    pc = {"blk": b, "rep": z * 2 + 1 - core}
    pz = [{"blk": b, "rep": lax.rem(z + k, nz) * 2 + core} for k in range(1, nz)]

    used = [0]

    def push(src, dst, dev):
        s = used[0]
        used[0] += 1
        copy = pltpu.make_async_remote_copy(
            src_ref=src, dst_ref=dst, send_sem=send.at[s], recv_sem=recv.at[s],
            device_id=dev, device_id_type=MESH,
        )
        copy.start()
        started.append(copy)
        return copy

    started = []
    barrier = pltpu.get_barrier_semaphore()
    for dev in [px, py, pc] + pz:
        pl.semaphore_signal(barrier, inc=1, device_id=dev, device_id_type=MESH)

    def project(c, feats, head, embed, factor, rounded):
        rows = pl.ds(c * chunk, chunk)
        raw = mm(feats[rows, :], head[...])
        f = lax.rsqrt(jnp.sum(raw * raw, axis=1, keepdims=True) + epsilon)
        out = raw * f
        embed[rows, :] = out
        factor[rows, :] = f
        rounded[rows, :] = out.astype(jnp.bfloat16)

    got_i, got_t = [], []
    for c in range(count):
        rows = pl.ds(c * chunk, chunk)
        project(c, xi, wi, ei, fi, im)
        if c == 0:
            pl.semaphore_wait(barrier, 2 + nz)
            got_li = push(li, lip, px)
            got_lt = push(lt, ltp, py)
        got_i.append(push(im.at[rows, :], ip.at[rows, :], px))
        project(c, xt, wt, et, ft, tm)
        got_t.append(push(tm.at[rows, :], tp.at[rows, :], py))

    def columns(lse):
        half = 0.5 * jnp.exp(-lse)
        return jnp.transpose(jnp.broadcast_to(half, (128, n)))

    u[0] = columns(li[...])
    v[0] = 0.5 * jnp.exp(-lt[...])
    images, texts = (im, ip), (tm, tp)

    def tile(p, q, r0, nr, c0, nc):
        s = logit_scale * mm(images[p][pl.ds(r0, nr), :], texts[q][pl.ds(c0, nc), :], NT)
        fac = u[p, pl.ds(r0, nr), :][:, :1] + v[q, :, pl.ds(c0, nc)]
        w[p, q, pl.ds(r0, nr), pl.ds(c0, nc)] = (jnp.exp(s) * fac).astype(jnp.bfloat16)

    @pl.loop(0, count)
    def _(c):
        tile(0, 0, pl.multiple_of(c * chunk, chunk), chunk, 0, n)

    @pl.loop(0, count)
    def _(c):
        rows = pl.ds(pl.multiple_of(c * chunk, chunk), chunk)
        acc_i[rows, :] = mm(w[0, 0, rows, :], tm[...])
        acc_t[rows, :] = mm(w[0, 0, :, rows], im[...], TN)

    for src, dst, width in ((xi, xit, di), (xt, xtt, dt)):

        @pl.loop(0, width // 128)
        def _(k, src=src, dst=dst):
            part = pl.ds(pl.multiple_of(k * 128, 128), 128)
            dst[part, :] = jnp.transpose(src[:, part])

    got_li.wait_recv()
    got_lt.wait_recv()
    u[1] = columns(lip[...])
    v[1] = 0.5 * jnp.exp(-ltp[...])
    for c in range(count):
        got_i[c].wait_recv()
        tile(1, 0, c * chunk, chunk, 0, n)
        got_t[c].wait_recv()

        tile(0, 1, 0, n, c * chunk, chunk)
        tile(1, 1, c * chunk, chunk, 0, (c + 1) * chunk)
        if c > 0:
            tile(1, 1, 0, c * chunk, c * chunk, chunk)

    sum_i, sum_t = [], []
    for c in range(count):
        rows = pl.ds(c * chunk, chunk)
        ps_i[rows, :] = (mm(w[1, 0, rows, :], tm[...]) + mm(w[1, 1, rows, :], tp[...])).astype(
            jnp.bfloat16
        )
        sum_i.append(push(ps_i.at[rows, :], pr_i.at[rows, :], px))
        ps_t[rows, :] = (
            mm(w[0, 1, :, rows], im[...], TN) + mm(w[1, 1, :, rows], ip[...], TN)
        ).astype(jnp.bfloat16)
        sum_t.append(push(ps_t.at[rows, :], pr_t.at[rows, :], py))

    @pl.loop(0, count)
    def _(c):
        rows = pl.ds(pl.multiple_of(c * chunk, chunk), chunk)
        acc_i[rows, :] += mm(w[0, 1, rows, :], tp[...])
        acc_t[rows, :] += mm(w[1, 0, :, rows], ip[...], TN)

    def finish(c, acc, part, other, embed, factor, out):
        rows = pl.ds(c * chunk, chunk)
        total = acc[rows, :] + part[rows, :].astype(jnp.float32)
        grad = logit_scale * total - logit_scale * other[rows, :].astype(jnp.float32)
        out[rows, :] = pre_gradient(embed[rows, :], factor[rows, :], grad)

    for c in range(count):
        sum_i[c].wait_recv()
        finish(c, acc_i, pr_i, tm, ei, fi, pre_i)
        sum_t[c].wait_recv()
        finish(c, acc_t, pr_t, im, et, ft, pre_t)

    eh = e // 2

    def added(p, q):
        return (p.astype(jnp.float32) + q.astype(jnp.float32)).astype(jnp.bfloat16)

    ij = ((x, y), (y, x))
    pi, pj = (px, py), (py, px)
    both = range(2)

    def head_half(which, dst, flipped, pre):
        part = dst.shape[4]
        half = flipped.shape[0] // 2
        for q in range(4):
            rows = pl.ds(pl.multiple_of(which * half + q * nz * part, nz * part), nz * part)
            g = mm(flipped[rows, :], pre[...])
            for ab in both:
                for k in range(nz):
                    dst[ab, q // 2, q % 2, k] = g[
                        k * part : (k + 1) * part, ab * eh : (ab + 1) * eh
                    ].astype(jnp.bfloat16)

    def reduce_head(flipped, pre, result, out_half, own, from_core, r1, r2, r3, full):
        head_half(1 - core, out_half, flipped, pre)
        first, second = [
            [push(out_half.at[ab, i], from_core.at[ab, i], pc) for ab, i in places]
            for places in (
                [(ab, 1 - ij[ab][0]) for ab in both],
                [(ab, ij[ab][0]) for ab in both],
            )
        ]
        head_half(core, own, flipped, pre)
        s1 = []
        for ab in both:
            i = ij[ab][0]
            first[ab].wait_recv()
            own[ab, 1 - i] = added(own[ab, 1 - i], from_core[ab, 1 - i])
            s1.append(push(own.at[ab, 1 - i], r1.at[ab], pi[ab]))
        for ab in both:
            i = ij[ab][0]
            second[ab].wait_recv()
            own[ab, i] = added(own[ab, i], from_core[ab, i])
        yield
        s2 = []
        for ab in both:
            i, j = ij[ab]
            s1[ab].wait_recv()
            own[ab, i] = added(own[ab, i], r1[ab])
            s2.append(push(own.at[ab, i, 1 - j], r2.at[ab], pj[ab]))
        yield
        s3 = []
        for ab in both:
            i, j = ij[ab]
            s2[ab].wait_recv()
            own[ab, i, j] = added(own[ab, i, j], r2[ab])
            s3.append(
                [push(own.at[ab, i, j, lax.rem(z + k, nz)], r3.at[ab, k], pz[k - 1]) for k in range(1, nz)]
            )
        yield
        s4 = []
        for ab in both:
            i, j = ij[ab]
            total = own[ab, i, j, z].astype(jnp.float32)
            for k in range(1, nz):
                s3[ab][k - 1].wait_recv()
                total = total + r3[ab, k].astype(jnp.float32)
            full[core, ab, i, j, z] = total.astype(jnp.bfloat16)
            piece = full.at[core, ab, i, j, z]
            s4.append([push(piece, piece, pz[k - 1]) for k in range(1, nz)])
        yield
        s5 = []
        for ab in both:
            i, j = ij[ab]
            for copy in s4[ab]:
                copy.wait_recv()
            piece = full.at[core, ab, i, j]
            s5.append(push(piece, piece, pj[ab]))
        yield
        s6, last = [], []
        for ab in both:
            i, j = ij[ab]
            s5[ab].wait_recv()
            piece = full.at[core, ab, i]
            s6.append(push(piece, piece, pi[ab]))
            last.append(push(piece, piece, pc))
        yield
        for ab in both:
            i, j = ij[ab]
            s6[ab].wait_recv()
            piece = full.at[core, ab, 1 - i]
            last.append(push(piece, piece, pc))
        for copy in last:
            copy.wait_recv()
        part = full.shape[5]
        for cc in both:
            for ab in both:
                for q in range(4):
                    for k in range(nz):
                        result[
                            pl.ds(((cc * 4 + q) * nz + k) * part, part), pl.ds(ab * eh, eh)
                        ] = full[cc, ab, q // 2, q % 2, k]
        yield

    parts = [reduce_head(xtt, pre_t, ht, *bufs_t), reduce_head(xit, pre_i, hi, *bufs_i)]
    for _ in range(7):
        for step in parts:
            next(step)
    for copy in started:
        copy.wait_send()


def kernel_shards(nz, image_feats, text_feats, image_head, text_head, image_lse, text_lse):
    n, di = image_feats.shape[1:]
    dt, e = text_head.shape
    chunk = n // 4
    bf, f32 = jnp.bfloat16, jnp.float32
    vm = pltpu.VMEM

    def buffers(rows):
        leads = [(2, 2, 2, nz)] * 3 + [(2, 2, nz), (2, nz), (2, nz), (2, 2, 2, 2, nz)]
        return [vm((*lead, rows // (8 * nz), e // 2), bf) for lead in leads]

    copies = 2 + 4 * (n // chunk) + 2 * (4 + 2 + 2 + 2 * (nz - 1) * 2 + 2 + 2 + 4)
    spec = pl.BlockSpec(memory_space=pltpu.VMEM)
    pre_i, pre_t, hi, ht = pl.pallas_call(
        functools.partial(fused, nz, chunk),
        out_shape=[
            jax.ShapeDtypeStruct((n, e), bf),
            jax.ShapeDtypeStruct((n, e), bf),
            jax.ShapeDtypeStruct((di, e), bf),
            jax.ShapeDtypeStruct((dt, e), bf),
        ],
        in_specs=[spec] * 6,
        out_specs=[spec] * 4,
        scratch_shapes=[
            vm((n, e), f32), vm((n, e), f32), vm((n, 1), f32), vm((n, 1), f32),
            vm((n, e), bf), vm((n, e), bf), vm((n, e), bf), vm((n, e), bf),
            vm((1, n), f32), vm((1, n), f32), vm((2, n, 128), f32), vm((2, 1, n), f32),
            vm((2, 2, n, n), bf),
            vm((n, e), bf), vm((n, e), bf), vm((n, e), bf), vm((n, e), bf),
            vm((n, e), f32), vm((n, e), f32), vm((di, n), bf), vm((dt, n), bf),
            buffers(di), buffers(dt),
            pltpu.SemaphoreType.DMA((copies,)), pltpu.SemaphoreType.DMA((copies,)),
        ],
        compiler_params=pltpu.CompilerParams(
            collective_id=0, has_side_effects=True, vmem_limit_bytes=60 * 1024 * 1024
        ),
    )(image_feats[0], text_feats[0], image_head, text_head, image_lse, text_lse)
    image_back = lax.dot_general(pre_i, image_head, NT, preferred_element_type=f32)
    text_back = lax.dot_general(pre_t, text_head, NT, preferred_element_type=f32)
    return (image_back[None], text_back[None], hi.astype(f32), ht.astype(f32))


def solution(mesh):
    blk, rep = mesh.shape["blk"], mesh.shape["rep"]
    body = shards
    if blk == SIDE * SIDE and rep % SIDE == 0:
        body = functools.partial(kernel_shards, rep // SIDE)
    return jax.shard_map(
        body,
        mesh=mesh,
        in_specs=(
            P("rep", "blk", None),
            P("rep", "blk", None),
            P(),
            P(),
            P("rep", "blk"),
            P("rep", "blk"),
        ),
        out_specs=(P("rep", "blk", None), P("rep", "blk", None), P(), P()),
        check_vma=False,
    )
```

```python
import functools

import jax
import jax.numpy as jnp
from jax import lax
from jax.experimental import pallas as pl
from jax.experimental.pallas import tpu as pltpu
from jax.sharding import PartitionSpec as P

logit_scale = 50.0
epsilon = 1e-06


def project_head(feats, weight):
    raw = jnp.dot(feats, weight, preferred_element_type=jnp.float32)
    factor = lax.rsqrt(jnp.sum(raw * raw, axis=1, keepdims=True) + epsilon)
    return (raw * factor, factor)


def pre_gradient(embed, factor, grad):
    inner = jnp.sum(embed * grad, axis=1, keepdims=True)
    return (factor * (grad - embed * inner)).astype(jnp.bfloat16)


def weight_tile(left, left_lse, right, right_lse):
    scores = logit_scale * lax.dot_general(
        left, right, (((1,), (1,)), ((), ())), preferred_element_type=jnp.float32
    )
    return (
        0.5 * (jnp.exp(scores - left_lse[:, None]) + jnp.exp(scores - right_lse[None, :]))
    ).astype(jnp.bfloat16)


def shards(image_feats, text_feats, image_head, text_head, image_lse, text_lse):
    image_rows = image_feats[0]
    text_rows = text_feats[0]
    lse_img = image_lse[0]
    lse_txt = text_lse[0]
    image_embed, image_scale = project_head(image_rows, image_head)
    text_embed, text_scale = project_head(text_rows, text_head)
    image_round = image_embed.astype(jnp.bfloat16)
    text_round = text_embed.astype(jnp.bfloat16)
    image_piece = lax.all_gather(image_round, "blk", axis=0, tiled=True)
    image_piece_lse = lax.all_gather(
        lse_img.astype(jnp.bfloat16), "blk", axis=0, tiled=True
    ).astype(jnp.float32)
    text_piece = lax.all_gather(text_round, "blk", axis=0, tiled=True)
    text_piece_lse = lax.all_gather(lse_txt.astype(jnp.bfloat16), "blk", axis=0, tiled=True).astype(
        jnp.float32
    )
    image_weights = weight_tile(image_round, lse_img, text_piece, text_piece_lse)
    image_total_part = jnp.dot(image_weights, text_piece, preferred_element_type=jnp.float32)
    text_weights = weight_tile(image_piece, image_piece_lse, text_round, lse_txt)
    text_total_part = lax.dot_general(
        text_weights, image_piece, (((0,), (0,)), ((), ())), preferred_element_type=jnp.float32
    )
    image_grad = logit_scale * image_total_part - logit_scale * text_round.astype(jnp.float32)
    text_grad = logit_scale * text_total_part - logit_scale * image_round.astype(jnp.float32)
    image_pre = pre_gradient(image_embed, image_scale, image_grad)
    text_pre = pre_gradient(text_embed, text_scale, text_grad)
    image_back = lax.dot_general(
        image_pre, image_head, (((1,), (1,)), ((), ())), preferred_element_type=jnp.float32
    )
    text_back = lax.dot_general(
        text_pre, text_head, (((1,), (1,)), ((), ())), preferred_element_type=jnp.float32
    )
    image_wgrad = lax.dot_general(
        image_rows, image_pre, (((0,), (0,)), ((), ())), preferred_element_type=jnp.float32
    )
    text_wgrad = lax.dot_general(
        text_rows, text_pre, (((0,), (0,)), ((), ())), preferred_element_type=jnp.float32
    )
    image_total, text_total = lax.psum((image_wgrad, text_wgrad), ("blk", "rep"))
    return (image_back[None], text_back[None], image_total, text_total)


MESH = pl.DeviceIdType.MESH
SIDE = 2
NT = (((1,), (1,)), ((), ()))
TN = (((0,), (0,)), ((), ()))


def mm(a, b, dims=(((1,), (0,)), ((), ()))):
    return lax.dot_general(a, b, dims, preferred_element_type=jnp.float32)


def fused(
    nz, chunk,
    xi_in, xt_in, wi_in, wt_in, li, lt,
    pre_i_out, pre_t_out, hi_out, ht_out,
    xi, xt, wi, wt, pre_i, pre_t, hi, ht,
    ei, et, fi, ft, im, ip, tm, tp, lip, ltp, u, v, w,
    ps_i, pr_i, ps_t, pr_t, acc_i, acc_t, xit, xtt,
    bufs_low, bufs_high, bufs_t,
    send, recv, local,
):
    n, e = im.shape
    di, dt = wi.shape[0], wt.shape[0]
    count = n // chunk
    b, r = lax.axis_index("blk"), lax.axis_index("rep")
    x, y = lax.rem(b, 2), b // 2
    core, z = lax.rem(r, 2), r // 2
    px = {"blk": y * 2 + 1 - x, "rep": r}
    py = {"blk": (1 - y) * 2 + x, "rep": r}
    pc = {"blk": b, "rep": z * 2 + 1 - core}
    pz = [{"blk": b, "rep": lax.rem(z + k, nz) * 2 + core} for k in range(1, nz)]

    used = [0]

    def push(src, dst, dev):
        s = used[0]
        used[0] += 1
        copy = pltpu.make_async_remote_copy(
            src_ref=src, dst_ref=dst, send_sem=send.at[s], recv_sem=recv.at[s],
            device_id=dev, device_id_type=MESH,
        )
        copy.start()
        started.append(copy)
        return copy

    started, moved = [], []

    def move(src, dst):
        copy = pltpu.make_async_copy(src, dst, local.at[len(moved)])
        copy.start()
        moved.append(copy)
        return copy

    def piece_of(c, feats_in, feats):
        rows = pl.ds(c * chunk, chunk)
        return move(feats_in.at[rows, :], feats.at[rows, :])

    in_wi = move(wi_in, wi)
    in_xi = [piece_of(0, xi_in, xi)]
    in_wt = move(wt_in, wt)
    in_xt = [piece_of(0, xt_in, xt)]
    for c in range(1, count):
        in_xi.append(piece_of(c, xi_in, xi))
        in_xt.append(piece_of(c, xt_in, xt))
    barrier = pltpu.get_barrier_semaphore()
    for dev in [px, py, pc] + pz:
        pl.semaphore_signal(barrier, inc=1, device_id=dev, device_id_type=MESH)

    def project(c, feats, head, embed, factor, rounded):
        rows = pl.ds(c * chunk, chunk)
        raw = mm(feats[rows, :], head[...])
        f = lax.rsqrt(jnp.sum(raw * raw, axis=1, keepdims=True) + epsilon)
        out = raw * f
        embed[rows, :] = out
        factor[rows, :] = f
        rounded[rows, :] = out.astype(jnp.bfloat16)

    got_i, got_t = [], []
    for c in range(count):
        rows = pl.ds(c * chunk, chunk)
        if c == 0:
            in_wi.wait()
        in_xi[c].wait()
        project(c, xi, wi, ei, fi, im)
        if c == 0:
            pl.semaphore_wait(barrier, 2 + nz)
            got_li = push(li, lip, px)
            got_lt = push(lt, ltp, py)
        got_i.append(push(im.at[rows, :], ip.at[rows, :], px))
        if c == 0:
            in_wt.wait()
        in_xt[c].wait()
        project(c, xt, wt, et, ft, tm)
        got_t.append(push(tm.at[rows, :], tp.at[rows, :], py))

    def columns(lse):
        half = 0.5 * jnp.exp(-lse)
        return jnp.transpose(jnp.broadcast_to(half, (128, n)))

    u[0] = columns(li[...])
    v[0] = 0.5 * jnp.exp(-lt[...])
    images, texts = (im, ip), (tm, tp)

    def tile(p, q, r0, nr, c0, nc):
        s = logit_scale * mm(images[p][pl.ds(r0, nr), :], texts[q][pl.ds(c0, nc), :], NT)
        fac = u[p, pl.ds(r0, nr), :][:, :1] + v[q, :, pl.ds(c0, nc)]
        w[p, q, pl.ds(r0, nr), pl.ds(c0, nc)] = (jnp.exp(s) * fac).astype(jnp.bfloat16)

    @pl.loop(0, count)
    def _(c):
        tile(0, 0, pl.multiple_of(c * chunk, chunk), chunk, 0, n)

    @pl.loop(0, count)
    def _(c):
        rows = pl.ds(pl.multiple_of(c * chunk, chunk), chunk)
        acc_i[rows, :] = mm(w[0, 0, rows, :], tm[...])
        acc_t[rows, :] = mm(w[0, 0, :, rows], im[...], TN)

    for src, dst, width in ((xi, xit, di), (xt, xtt, dt)):

        @pl.loop(0, width // 128)
        def _(k, src=src, dst=dst):
            part = pl.ds(pl.multiple_of(k * 128, 128), 128)
            dst[part, :] = jnp.transpose(src[:, part])

    got_li.wait_recv()
    got_lt.wait_recv()
    u[1] = columns(lip[...])
    v[1] = 0.5 * jnp.exp(-ltp[...])
    for c in range(count):
        got_i[c].wait_recv()
        tile(1, 0, c * chunk, chunk, 0, n)
        got_t[c].wait_recv()

        tile(0, 1, 0, n, c * chunk, chunk)
        tile(1, 1, c * chunk, chunk, 0, (c + 1) * chunk)
        if c > 0:
            tile(1, 1, 0, c * chunk, c * chunk, chunk)

    sum_i, sum_t = [], []
    for c in range(count):
        rows = pl.ds(c * chunk, chunk)
        ps_i[rows, :] = (mm(w[1, 0, rows, :], tm[...]) + mm(w[1, 1, rows, :], tp[...])).astype(
            jnp.bfloat16
        )
        sum_i.append(push(ps_i.at[rows, :], pr_i.at[rows, :], px))
        ps_t[rows, :] = (
            mm(w[0, 1, :, rows], im[...], TN) + mm(w[1, 1, :, rows], ip[...], TN)
        ).astype(jnp.bfloat16)
        sum_t.append(push(ps_t.at[rows, :], pr_t.at[rows, :], py))

    @pl.loop(0, count)
    def _(c):
        rows = pl.ds(pl.multiple_of(c * chunk, chunk), chunk)
        acc_i[rows, :] += mm(w[0, 1, rows, :], tp[...])
        acc_t[rows, :] += mm(w[1, 0, :, rows], ip[...], TN)

    def finish(c, acc, part, other, embed, factor, out):
        rows = pl.ds(c * chunk, chunk)
        total = acc[rows, :] + part[rows, :].astype(jnp.float32)
        grad = logit_scale * total - logit_scale * other[rows, :].astype(jnp.float32)
        out[rows, :] = pre_gradient(embed[rows, :], factor[rows, :], grad)

    for c in range(count):
        sum_i[c].wait_recv()
        finish(c, acc_i, pr_i, tm, ei, fi, pre_i)
        sum_t[c].wait_recv()
        finish(c, acc_t, pr_t, im, et, ft, pre_t)

    outputs = [move(pre_i, pre_i_out), move(pre_t, pre_t_out)]
    eh = e // 2

    def added(p, q):
        return (p.astype(jnp.float32) + q.astype(jnp.float32)).astype(jnp.bfloat16)

    ij = ((x, y), (y, x))
    pi, pj = (px, py), (py, px)
    both = range(2)

    def head_half(which, dst, flipped, pre):
        part = dst.shape[4]
        half = flipped.shape[0] // 2
        for q in range(4):
            rows = pl.ds(pl.multiple_of(which * half + q * nz * part, nz * part), nz * part)
            g = mm(flipped[rows, :], pre[...])
            for ab in both:
                for k in range(nz):
                    dst[ab, q // 2, q % 2, k] = g[
                        k * part : (k + 1) * part, ab * eh : (ab + 1) * eh
                    ].astype(jnp.bfloat16)

    def reduce_head(flipped, pre, result, result_out, out_half, own, from_core, r1, r2, r3, full):
        head_half(1 - core, out_half, flipped, pre)
        first, second = [
            [push(out_half.at[ab, i], from_core.at[ab, i], pc) for ab, i in places]
            for places in (
                [(ab, 1 - ij[ab][0]) for ab in both],
                [(ab, ij[ab][0]) for ab in both],
            )
        ]
        head_half(core, own, flipped, pre)
        s1 = []
        for ab in both:
            i = ij[ab][0]
            first[ab].wait_recv()
            own[ab, 1 - i] = added(own[ab, 1 - i], from_core[ab, 1 - i])
            s1.append(push(own.at[ab, 1 - i], r1.at[ab], pi[ab]))
        for ab in both:
            i = ij[ab][0]
            second[ab].wait_recv()
            own[ab, i] = added(own[ab, i], from_core[ab, i])
        yield
        s2 = []
        for ab in both:
            i, j = ij[ab]
            s1[ab].wait_recv()
            own[ab, i] = added(own[ab, i], r1[ab])
            s2.append(push(own.at[ab, i, 1 - j], r2.at[ab], pj[ab]))
        yield
        s3 = []
        for ab in both:
            i, j = ij[ab]
            s2[ab].wait_recv()
            own[ab, i, j] = added(own[ab, i, j], r2[ab])
            s3.append(
                [push(own.at[ab, i, j, lax.rem(z + k, nz)], r3.at[ab, k], pz[k - 1]) for k in range(1, nz)]
            )
        yield
        s4 = []
        for ab in both:
            i, j = ij[ab]
            total = own[ab, i, j, z].astype(jnp.float32)
            for k in range(1, nz):
                s3[ab][k - 1].wait_recv()
                total = total + r3[ab, k].astype(jnp.float32)
            full[core, ab, i, j, z] = total.astype(jnp.bfloat16)
            piece = full.at[core, ab, i, j, z]
            s4.append([push(piece, piece, pz[k - 1]) for k in range(1, nz)])
        yield
        s5 = []
        for ab in both:
            i, j = ij[ab]
            for copy in s4[ab]:
                copy.wait_recv()
            piece = full.at[core, ab, i, j]
            s5.append(push(piece, piece, pj[ab]))
        yield
        s6, last = [], []
        for ab in both:
            i, j = ij[ab]
            s5[ab].wait_recv()
            piece = full.at[core, ab, i]
            s6.append(push(piece, piece, pi[ab]))
            last.append(push(piece, piece, pc))
        yield
        for ab in both:
            i, j = ij[ab]
            s6[ab].wait_recv()
            piece = full.at[core, ab, 1 - i]
            last.append(push(piece, piece, pc))
        for copy in last:
            copy.wait_recv()
        part = full.shape[5]
        for cc in both:
            for ab in both:
                for q in range(4):
                    for k in range(nz):
                        result[
                            pl.ds(((cc * 4 + q) * nz + k) * part, part), pl.ds(ab * eh, eh)
                        ] = full[cc, ab, q // 2, q % 2, k]
        outputs.append(move(result, result_out))
        yield

    low, high = pl.ds(0, di // 2), pl.ds(di // 2, di // 2)
    parts = [
        reduce_head(xit.at[low, :], pre_i, hi.at[low, :], hi_out.at[low, :], *bufs_low),
        reduce_head(xit.at[high, :], pre_i, hi.at[high, :], hi_out.at[high, :], *bufs_high),
        reduce_head(xtt, pre_t, ht, ht_out, *bufs_t),
    ]
    for _ in range(7):
        for step in parts:
            next(step)
    for copy in outputs:
        copy.wait()
    for copy in started:
        copy.wait_send()


def kernel_shards(nz, image_feats, text_feats, image_head, text_head, image_lse, text_lse):
    n, di = image_feats.shape[1:]
    dt, e = text_head.shape
    chunk = n // 4
    bf, f32 = jnp.bfloat16, jnp.float32
    vm = pltpu.VMEM

    def buffers(rows):
        leads = [(2, 2, 2, nz)] * 3 + [(2, 2, nz), (2, nz), (2, nz), (2, 2, 2, 2, nz)]
        return [vm((*lead, rows // (8 * nz), e // 2), bf) for lead in leads]

    copies = 2 + 4 * (n // chunk) + 3 * (4 + 2 + 2 + 2 * (nz - 1) * 2 + 2 + 2 + 4)
    spec = pl.BlockSpec(memory_space=pltpu.VMEM)
    anywhere = pl.BlockSpec(memory_space=pl.ANY)
    pre_i, pre_t, hi, ht = pl.pallas_call(
        functools.partial(fused, nz, chunk),
        out_shape=[
            jax.ShapeDtypeStruct((n, e), bf),
            jax.ShapeDtypeStruct((n, e), bf),
            jax.ShapeDtypeStruct((di, e), bf),
            jax.ShapeDtypeStruct((dt, e), bf),
        ],
        in_specs=[anywhere] * 4 + [spec] * 2,
        out_specs=[anywhere] * 4,
        scratch_shapes=[
            vm((n, di), bf), vm((n, dt), bf), vm((di, e), bf), vm((dt, e), bf),
            vm((n, e), bf), vm((n, e), bf), vm((di, e), bf), vm((dt, e), bf),
            vm((n, e), f32), vm((n, e), f32), vm((n, 1), f32), vm((n, 1), f32),
            vm((n, e), bf), vm((n, e), bf), vm((n, e), bf), vm((n, e), bf),
            vm((1, n), f32), vm((1, n), f32), vm((2, n, 128), f32), vm((2, 1, n), f32),
            vm((2, 2, n, n), bf),
            vm((n, e), bf), vm((n, e), bf), vm((n, e), bf), vm((n, e), bf),
            vm((n, e), f32), vm((n, e), f32), vm((di, n), bf), vm((dt, n), bf),
            buffers(di // 2), buffers(di // 2), buffers(dt),
            pltpu.SemaphoreType.DMA((copies,)), pltpu.SemaphoreType.DMA((copies,)),
            pltpu.SemaphoreType.DMA((2 + 2 * (n // chunk) + 5,)),
        ],
        compiler_params=pltpu.CompilerParams(
            collective_id=0, has_side_effects=True, vmem_limit_bytes=60 * 1024 * 1024
        ),
    )(image_feats[0], text_feats[0], image_head, text_head, image_lse, text_lse)
    image_back = lax.dot_general(pre_i, image_head, NT, preferred_element_type=f32)
    text_back = lax.dot_general(pre_t, text_head, NT, preferred_element_type=f32)
    return (image_back[None], text_back[None], hi.astype(f32), ht.astype(f32))


def solution(mesh):
    blk, rep = mesh.shape["blk"], mesh.shape["rep"]
    body = shards
    if blk == SIDE * SIDE and rep % SIDE == 0:
        body = functools.partial(kernel_shards, rep // SIDE)
    return jax.shard_map(
        body,
        mesh=mesh,
        in_specs=(
            P("rep", "blk", None),
            P("rep", "blk", None),
            P(),
            P(),
            P("rep", "blk"),
            P("rep", "blk"),
        ),
        out_specs=(P("rep", "blk", None), P("rep", "blk", None), P(), P()),
        check_vma=False,
    )
```

```python
import functools

import jax
import jax.numpy as jnp
from jax import lax
from jax.experimental import pallas as pl
from jax.experimental.pallas import tpu as pltpu
from jax.sharding import PartitionSpec as P

logit_scale = 50.0
epsilon = 1e-06


def project_head(feats, weight):
    raw = jnp.dot(feats, weight, preferred_element_type=jnp.float32)
    factor = lax.rsqrt(jnp.sum(raw * raw, axis=1, keepdims=True) + epsilon)
    return (raw * factor, factor)


def pre_gradient(embed, factor, grad):
    inner = jnp.sum(embed * grad, axis=1, keepdims=True)
    return (factor * (grad - embed * inner)).astype(jnp.bfloat16)


def weight_tile(left, left_lse, right, right_lse):
    scores = logit_scale * lax.dot_general(
        left, right, (((1,), (1,)), ((), ())), preferred_element_type=jnp.float32
    )
    return (
        0.5 * (jnp.exp(scores - left_lse[:, None]) + jnp.exp(scores - right_lse[None, :]))
    ).astype(jnp.bfloat16)


def shards(image_feats, text_feats, image_head, text_head, image_lse, text_lse):
    image_rows = image_feats[0]
    text_rows = text_feats[0]
    lse_img = image_lse[0]
    lse_txt = text_lse[0]
    image_embed, image_scale = project_head(image_rows, image_head)
    text_embed, text_scale = project_head(text_rows, text_head)
    image_round = image_embed.astype(jnp.bfloat16)
    text_round = text_embed.astype(jnp.bfloat16)
    image_piece = lax.all_gather(image_round, "blk", axis=0, tiled=True)
    image_piece_lse = lax.all_gather(
        lse_img.astype(jnp.bfloat16), "blk", axis=0, tiled=True
    ).astype(jnp.float32)
    text_piece = lax.all_gather(text_round, "blk", axis=0, tiled=True)
    text_piece_lse = lax.all_gather(lse_txt.astype(jnp.bfloat16), "blk", axis=0, tiled=True).astype(
        jnp.float32
    )
    image_weights = weight_tile(image_round, lse_img, text_piece, text_piece_lse)
    image_total_part = jnp.dot(image_weights, text_piece, preferred_element_type=jnp.float32)
    text_weights = weight_tile(image_piece, image_piece_lse, text_round, lse_txt)
    text_total_part = lax.dot_general(
        text_weights, image_piece, (((0,), (0,)), ((), ())), preferred_element_type=jnp.float32
    )
    image_grad = logit_scale * image_total_part - logit_scale * text_round.astype(jnp.float32)
    text_grad = logit_scale * text_total_part - logit_scale * image_round.astype(jnp.float32)
    image_pre = pre_gradient(image_embed, image_scale, image_grad)
    text_pre = pre_gradient(text_embed, text_scale, text_grad)
    image_back = lax.dot_general(
        image_pre, image_head, (((1,), (1,)), ((), ())), preferred_element_type=jnp.float32
    )
    text_back = lax.dot_general(
        text_pre, text_head, (((1,), (1,)), ((), ())), preferred_element_type=jnp.float32
    )
    image_wgrad = lax.dot_general(
        image_rows, image_pre, (((0,), (0,)), ((), ())), preferred_element_type=jnp.float32
    )
    text_wgrad = lax.dot_general(
        text_rows, text_pre, (((0,), (0,)), ((), ())), preferred_element_type=jnp.float32
    )
    image_total, text_total = lax.psum((image_wgrad, text_wgrad), ("blk", "rep"))
    return (image_back[None], text_back[None], image_total, text_total)


MESH = pl.DeviceIdType.MESH
SIDE = 2
NT = (((1,), (1,)), ((), ()))
TN = (((0,), (0,)), ((), ()))


def mm(a, b, dims=(((1,), (0,)), ((), ()))):
    return lax.dot_general(a, b, dims, preferred_element_type=jnp.float32)


def fused(
    nz, chunk,
    xi_in, xt_in, wi_in, wt_in, li, lt,
    pre_i_out, pre_t_out, hi_out, ht_out,
    xi, xt, wi, wt, pre_i, pre_t, hi, ht,
    ei, et, fi, ft, im, ip, tm, tp, lip, ltp, u, v, w,
    ps_i, pr_i, ps_t, pr_t, acc_i, acc_t, xit, xtt,
    bufs_low, bufs_high, bufs_t,
    send, recv, local,
):
    n, e = im.shape
    di, dt = wi.shape[0], wt.shape[0]
    count = n // chunk
    b, r = lax.axis_index("blk"), lax.axis_index("rep")
    x, y = lax.rem(b, 2), b // 2
    core, z = lax.rem(r, 2), r // 2
    px = {"blk": y * 2 + 1 - x, "rep": r}
    py = {"blk": (1 - y) * 2 + x, "rep": r}
    pc = {"blk": b, "rep": z * 2 + 1 - core}
    pz = [{"blk": b, "rep": lax.rem(z + k, nz) * 2 + core} for k in range(1, nz)]

    used = [0]

    def push(src, dst, dev):
        s = used[0]
        used[0] += 1
        copy = pltpu.make_async_remote_copy(
            src_ref=src, dst_ref=dst, send_sem=send.at[s], recv_sem=recv.at[s],
            device_id=dev, device_id_type=MESH,
        )
        copy.start()
        started.append(copy)
        return copy

    started, moved = [], []

    def move(src, dst):
        copy = pltpu.make_async_copy(src, dst, local.at[len(moved)])
        copy.start()
        moved.append(copy)
        return copy

    def piece_of(c, feats_in, feats):
        rows = pl.ds(c * chunk, chunk)
        return move(feats_in.at[rows, :], feats.at[rows, :])

    in_wi = move(wi_in, wi)
    in_xi = [piece_of(0, xi_in, xi)]
    in_wt = move(wt_in, wt)
    in_xt = [piece_of(0, xt_in, xt)]
    for c in range(1, count):
        in_xi.append(piece_of(c, xi_in, xi))
        in_xt.append(piece_of(c, xt_in, xt))
    barrier = pltpu.get_barrier_semaphore()
    for dev in [px, py, pc] + pz:
        pl.semaphore_signal(barrier, inc=1, device_id=dev, device_id_type=MESH)

    def project(c, feats, head, embed, factor, rounded):
        rows = pl.ds(c * chunk, chunk)
        raw = mm(feats[rows, :], head[...])
        f = lax.rsqrt(jnp.sum(raw * raw, axis=1, keepdims=True) + epsilon)
        out = raw * f
        embed[rows, :] = out
        factor[rows, :] = f
        rounded[rows, :] = out.astype(jnp.bfloat16)

    got_i, got_t = [], []
    for c in range(count):
        rows = pl.ds(c * chunk, chunk)
        if c == 0:
            in_wi.wait()
        in_xi[c].wait()
        project(c, xi, wi, ei, fi, im)
        if c == 0:
            pl.semaphore_wait(barrier, 2 + nz)
            got_li = push(li, lip, px)
            got_lt = push(lt, ltp, py)
        got_i.append(push(im.at[rows, :], ip.at[rows, :], px))
        if c == 0:
            in_wt.wait()
        in_xt[c].wait()
        project(c, xt, wt, et, ft, tm)
        got_t.append(push(tm.at[rows, :], tp.at[rows, :], py))

    def columns(lse):
        half = 0.5 * jnp.exp(-lse)
        return jnp.transpose(jnp.broadcast_to(half, (128, n)))

    u[0] = columns(li[...])
    v[0] = 0.5 * jnp.exp(-lt[...])
    images, texts = (im, ip), (tm, tp)

    def tile(p, q, r0, nr, c0, nc):
        s = logit_scale * mm(images[p][pl.ds(r0, nr), :], texts[q][pl.ds(c0, nc), :], NT)
        fac = u[p, pl.ds(r0, nr), :][:, :1] + v[q, :, pl.ds(c0, nc)]
        w[p, q, pl.ds(r0, nr), pl.ds(c0, nc)] = (jnp.exp(s) * fac).astype(jnp.bfloat16)

    @pl.loop(0, count)
    def _(c):
        tile(0, 0, pl.multiple_of(c * chunk, chunk), chunk, 0, n)

    @pl.loop(0, count)
    def _(c):
        rows = pl.ds(pl.multiple_of(c * chunk, chunk), chunk)
        acc_i[rows, :] = mm(w[0, 0, rows, :], tm[...])
        acc_t[rows, :] = mm(w[0, 0, :, rows], im[...], TN)

    for src, dst, width in ((xi, xit, di), (xt, xtt, dt)):

        @pl.loop(0, width // 128)
        def _(k, src=src, dst=dst):
            part = pl.ds(pl.multiple_of(k * 128, 128), 128)
            dst[part, :] = jnp.transpose(src[:, part])

    got_li.wait_recv()
    got_lt.wait_recv()
    u[1] = columns(lip[...])
    v[1] = 0.5 * jnp.exp(-ltp[...])
    for c in range(count):
        got_i[c].wait_recv()
        tile(1, 0, c * chunk, chunk, 0, n)
        got_t[c].wait_recv()

        tile(0, 1, 0, n, c * chunk, chunk)
        tile(1, 1, c * chunk, chunk, 0, (c + 1) * chunk)
        if c > 0:
            tile(1, 1, 0, c * chunk, c * chunk, chunk)

    sum_i, sum_t = [], []
    for c in range(count):
        rows = pl.ds(c * chunk, chunk)
        ps_i[rows, :] = (mm(w[1, 0, rows, :], tm[...]) + mm(w[1, 1, rows, :], tp[...])).astype(
            jnp.bfloat16
        )
        sum_i.append(push(ps_i.at[rows, :], pr_i.at[rows, :], px))
        ps_t[rows, :] = (
            mm(w[0, 1, :, rows], im[...], TN) + mm(w[1, 1, :, rows], ip[...], TN)
        ).astype(jnp.bfloat16)
        sum_t.append(push(ps_t.at[rows, :], pr_t.at[rows, :], py))

    @pl.loop(0, count)
    def _(c):
        rows = pl.ds(pl.multiple_of(c * chunk, chunk), chunk)
        acc_i[rows, :] += mm(w[0, 1, rows, :], tp[...])
        acc_t[rows, :] += mm(w[1, 0, :, rows], ip[...], TN)

    def finish(c, acc, part, other, embed, factor, out):
        rows = pl.ds(c * chunk, chunk)
        total = acc[rows, :] + part[rows, :].astype(jnp.float32)
        grad = logit_scale * total - logit_scale * other[rows, :].astype(jnp.float32)
        out[rows, :] = pre_gradient(embed[rows, :], factor[rows, :], grad)

    for c in range(count):
        sum_i[c].wait_recv()
        finish(c, acc_i, pr_i, tm, ei, fi, pre_i)
        sum_t[c].wait_recv()
        finish(c, acc_t, pr_t, im, et, ft, pre_t)

    outputs = [move(pre_i, pre_i_out), move(pre_t, pre_t_out)]
    eh = e // 2

    def added(p, q):
        return (p.astype(jnp.float32) + q.astype(jnp.float32)).astype(jnp.bfloat16)

    ij = ((x, y), (y, x))
    pi, pj = (px, py), (py, px)
    both = range(2)

    def head_half(which, dst, flipped, pre):
        part = dst.shape[4]
        half = flipped.shape[0] // 2
        for q in range(4):
            rows = pl.ds(pl.multiple_of(which * half + q * nz * part, nz * part), nz * part)
            g = mm(flipped[rows, :], pre[...])
            for ab in both:
                for k in range(nz):
                    dst[ab, q // 2, q % 2, k] = g[
                        k * part : (k + 1) * part, ab * eh : (ab + 1) * eh
                    ].astype(jnp.bfloat16)

    def reduce_head(flipped, pre, result, result_out, out_half, own, from_core, r1, r2, r3, full):
        head_half(1 - core, out_half, flipped, pre)
        first, second = [
            [push(out_half.at[ab, i], from_core.at[ab, i], pc) for ab, i in places]
            for places in (
                [(ab, 1 - ij[ab][0]) for ab in both],
                [(ab, ij[ab][0]) for ab in both],
            )
        ]
        head_half(core, own, flipped, pre)
        s1 = []
        for ab in both:
            i = ij[ab][0]
            first[ab].wait_recv()
            own[ab, 1 - i] = added(own[ab, 1 - i], from_core[ab, 1 - i])
            s1.append(push(own.at[ab, 1 - i], r1.at[ab], pi[ab]))
        for ab in both:
            i = ij[ab][0]
            second[ab].wait_recv()
            own[ab, i] = added(own[ab, i], from_core[ab, i])
        yield
        s2 = []
        for ab in both:
            i, j = ij[ab]
            s1[ab].wait_recv()
            own[ab, i] = added(own[ab, i], r1[ab])
            s2.append(push(own.at[ab, i, 1 - j], r2.at[ab], pj[ab]))
        yield
        s3 = []
        for ab in both:
            i, j = ij[ab]
            s2[ab].wait_recv()
            own[ab, i, j] = added(own[ab, i, j], r2[ab])
            s3.append(
                [push(own.at[ab, i, j, lax.rem(z + k, nz)], r3.at[ab, k], pz[k - 1]) for k in range(1, nz)]
            )
        yield
        s4 = []
        for ab in both:
            i, j = ij[ab]
            total = own[ab, i, j, z].astype(jnp.float32)
            for k in range(1, nz):
                s3[ab][k - 1].wait_recv()
                total = total + r3[ab, k].astype(jnp.float32)
            full[core, ab, i, j, z] = total.astype(jnp.bfloat16)
            piece = full.at[core, ab, i, j, z]
            s4.append([push(piece, piece, pz[k - 1]) for k in range(1, nz)])
        yield
        s5 = []
        for ab in both:
            i, j = ij[ab]
            for copy in s4[ab]:
                copy.wait_recv()
            piece = full.at[core, ab, i, j]
            s5.append(push(piece, piece, pj[ab]))
        yield
        s6, last = [], []
        for ab in both:
            i, j = ij[ab]
            s5[ab].wait_recv()
            piece = full.at[core, ab, i]
            s6.append(push(piece, piece, pi[ab]))
            last.append(push(piece, piece, pc))
        yield
        for ab in both:
            i, j = ij[ab]
            s6[ab].wait_recv()
            piece = full.at[core, ab, 1 - i]
            last.append(push(piece, piece, pc))
        for copy in last:
            copy.wait_recv()
        part = full.shape[5]
        for cc in both:
            for ab in both:
                for q in range(4):
                    for k in range(nz):
                        result[
                            pl.ds(((cc * 4 + q) * nz + k) * part, part), pl.ds(ab * eh, eh)
                        ] = full[cc, ab, q // 2, q % 2, k]
        outputs.append(move(result, result_out))
        yield

    low, high = pl.ds(0, di // 2), pl.ds(di // 2, di // 2)
    parts = [
        reduce_head(xit.at[low, :], pre_i, hi.at[low, :], hi_out.at[low, :], *bufs_low),
        reduce_head(xit.at[high, :], pre_i, hi.at[high, :], hi_out.at[high, :], *bufs_high),
        reduce_head(xtt, pre_t, ht, ht_out, *bufs_t),
    ]
    for _ in range(7):
        for step in parts:
            next(step)
    for copy in outputs:
        copy.wait()
    for copy in started:
        copy.wait_send()


def tail(pi, pt, wi, wt, hi, ht, bi, bt, gi, gt):
    bi[...] = mm(pi[...], wi[...], NT)
    bt[...] = mm(pt[...], wt[...], NT)
    gi[...] = hi[...].astype(jnp.float32)
    gt[...] = ht[...].astype(jnp.float32)


def kernel_shards(nz, image_feats, text_feats, image_head, text_head, image_lse, text_lse):
    n, di = image_feats.shape[1:]
    dt, e = text_head.shape
    chunk = n // 4
    bf, f32 = jnp.bfloat16, jnp.float32
    vm = pltpu.VMEM

    def buffers(rows):
        leads = [(2, 2, 2, nz)] * 3 + [(2, 2, nz), (2, nz), (2, nz), (2, 2, 2, 2, nz)]
        return [vm((*lead, rows // (8 * nz), e // 2), bf) for lead in leads]

    copies = 2 + 4 * (n // chunk) + 3 * (4 + 2 + 2 + 2 * (nz - 1) * 2 + 2 + 2 + 4)
    spec = pl.BlockSpec(memory_space=pltpu.VMEM)
    anywhere = pl.BlockSpec(memory_space=pl.ANY)
    pre_i, pre_t, hi, ht = pl.pallas_call(
        functools.partial(fused, nz, chunk),
        out_shape=[
            jax.ShapeDtypeStruct((n, e), bf),
            jax.ShapeDtypeStruct((n, e), bf),
            jax.ShapeDtypeStruct((di, e), bf),
            jax.ShapeDtypeStruct((dt, e), bf),
        ],
        in_specs=[anywhere] * 4 + [spec] * 2,
        out_specs=[anywhere] * 4,
        scratch_shapes=[
            vm((n, di), bf), vm((n, dt), bf), vm((di, e), bf), vm((dt, e), bf),
            vm((n, e), bf), vm((n, e), bf), vm((di, e), bf), vm((dt, e), bf),
            vm((n, e), f32), vm((n, e), f32), vm((n, 1), f32), vm((n, 1), f32),
            vm((n, e), bf), vm((n, e), bf), vm((n, e), bf), vm((n, e), bf),
            vm((1, n), f32), vm((1, n), f32), vm((2, n, 128), f32), vm((2, 1, n), f32),
            vm((2, 2, n, n), bf),
            vm((n, e), bf), vm((n, e), bf), vm((n, e), bf), vm((n, e), bf),
            vm((n, e), f32), vm((n, e), f32), vm((di, n), bf), vm((dt, n), bf),
            buffers(di // 2), buffers(di // 2), buffers(dt),
            pltpu.SemaphoreType.DMA((copies,)), pltpu.SemaphoreType.DMA((copies,)),
            pltpu.SemaphoreType.DMA((2 + 2 * (n // chunk) + 5,)),
        ],
        compiler_params=pltpu.CompilerParams(
            collective_id=0, has_side_effects=True, vmem_limit_bytes=60 * 1024 * 1024
        ),
    )(image_feats[0], text_feats[0], image_head, text_head, image_lse, text_lse)
    steps = 4

    def rows_of(total, width):
        return pl.BlockSpec((total // steps, width), lambda k: (k, 0))

    def whole(total):
        return pl.BlockSpec((total, e), lambda k: (0, 0))

    image_back, text_back, image_total, text_total = pl.pallas_call(
        tail,
        grid=(steps,),
        out_shape=[
            jax.ShapeDtypeStruct((n, di), f32),
            jax.ShapeDtypeStruct((n, dt), f32),
            jax.ShapeDtypeStruct((di, e), f32),
            jax.ShapeDtypeStruct((dt, e), f32),
        ],
        in_specs=[rows_of(n, e), rows_of(n, e), whole(di), whole(dt), rows_of(di, e), rows_of(dt, e)],
        out_specs=[rows_of(n, di), rows_of(n, dt), rows_of(di, e), rows_of(dt, e)],
        compiler_params=pltpu.CompilerParams(vmem_limit_bytes=60 * 1024 * 1024),
    )(pre_i, pre_t, image_head, text_head, hi, ht)
    return (image_back[None], text_back[None], image_total, text_total)


def solution(mesh):
    blk, rep = mesh.shape["blk"], mesh.shape["rep"]
    body = shards
    if blk == SIDE * SIDE and rep % SIDE == 0:
        body = functools.partial(kernel_shards, rep // SIDE)
    return jax.shard_map(
        body,
        mesh=mesh,
        in_specs=(
            P("rep", "blk", None),
            P("rep", "blk", None),
            P(),
            P(),
            P("rep", "blk"),
            P("rep", "blk"),
        ),
        out_specs=(P("rep", "blk", None), P("rep", "blk", None), P(), P()),
        check_vma=False,
    )
```
